32 devices in a mesh: replica: 16 (over z, y, core), fsdp: 2 (over x).
Axes of the slice: x: 2, y: 2, z: 4, core: 2. Of those that a mesh axis runs over, the one named last changes fastest.
Arguments:
- inner_weights: float32 [16, 3, 24, 6144], P('replica', None, None, 'fsdp'), may hold values from -8 to 8
- anchor: float32 [3, 24, 6144], P(None, None, 'fsdp'), may hold values from -4 to 4
- outer_moment: float32 [3, 24, 6144], P(None, None, 'fsdp'), may hold values from -3 to 3
- adam_first: float32 [16, 3, 24, 6144], P('replica', None, None, 'fsdp'), may hold values from -2 to 2
- adam_second: float32 [16, 3, 24, 6144], P('replica', None, None, 'fsdp'), may hold values from 0.1 to 1
- grad_parts: bfloat16 [16, 2, 3, 24, 6144], P('replica', 'fsdp'), may hold values from -2.5 to 2.5
Outputs:
- fresh_weights: bfloat16 [3, 24, 6144], replicated
- anchor_new: float32 [3, 24, 6144], P(None, None, 'fsdp')
- moment_new: float32 [3, 24, 6144], P(None, None, 'fsdp')
- first_new: float32 [16, 3, 24, 6144], P('replica', None, None, 'fsdp')
- second_new: float32 [16, 3, 24, 6144], P('replica', None, None, 'fsdp')
The draws below stay inside these ranges and needn't reach their ends.
All inputs are finite; a program needn't handle non-finite values.
Results may differ from the reference program's by a relative error of at most 0.0025.
Values may be sent and summed in bfloat16 or wider, within the bound.
A program may use at most 64 MiB of HBM per device.

```python
import math
import jax
import jax.numpy as jnp
from jax import lax

D = 6144
LAYERS = 3
ROWS = 24
REPLICAS = 16
GROUP = 2


def shared_anchor(key):
    inner_key = jax.random.fold_in(key, 11)
    return jnp.clip(jax.random.normal(inner_key, (LAYERS, ROWS, D), jnp.float32), -4.0, 4.0)


def draw_anchor(key, part):
    return shared_anchor(key)


def draw_inner_weights(key, part):
    drift_key = jax.random.fold_in(key, 12)
    drift = jnp.clip(jax.random.normal(drift_key, (REPLICAS, LAYERS, ROWS, D), jnp.float32), -4.0, 4.0)
    return shared_anchor(key)[None] + drift


def draw_grad_parts(key, part):
    common_key = jax.random.fold_in(key, 21)
    noise_key = jax.random.fold_in(key, 22)
    common = jnp.clip(jax.random.normal(common_key, (LAYERS, ROWS, D), jnp.float32), -4.0, 4.0)
    noise = jnp.clip(jax.random.normal(noise_key, (REPLICAS, GROUP, LAYERS, ROWS, D), jnp.float32), -4.0, 4.0)
    return (0.25 * (common[None, None] + noise)).astype(jnp.bfloat16)


def steps_of(stream_key, dims, shards, least, top_value):
    def one(dim, blocks):
        heights = jax.random.uniform(jax.random.fold_in(jax.random.fold_in(stream_key, 6), dim), (blocks,), jnp.float32, least / len(shards), top_value / len(shards))
        return jnp.repeat(jnp.exp(heights), dims[dim] // blocks).reshape((-1,) + (1,) * (len(dims) - dim - 1))

    loudness = one(*shards[0])
    for cut in shards[1:]:
        loudness = loudness * one(*cut)
    return loudness


def scatter_about(key, extent, width, bound, shards=(), dtype=jnp.bfloat16):
    gain = steps_of(key, extent, shards, -0.22, 0.18) if shards else 1.0
    drawn = jax.random.normal(key, extent, jnp.float32) * width * gain
    return jnp.minimum(jnp.maximum(drawn, -bound), bound).astype(dtype)


def setup_inputs(seed: int = 0) -> dict:
    key_of = jax.random.split(jax.random.key(seed), 7)
    return {
        "inner_weights": draw_inner_weights(jax.random.fold_in(key_of[6], 71), 0),
        "anchor": draw_anchor(jax.random.fold_in(key_of[6], 71), 0),
        "outer_moment": scatter_about(key_of[2], (LAYERS, ROWS, D), 0.5, 3.0, ((2, 2),), jnp.float32),
        "adam_first": scatter_about(key_of[3], (REPLICAS, LAYERS, ROWS, D), 0.3, 2.0, ((0, 16), (3, 2)), jnp.float32),
        "adam_second": jnp.clip(jnp.exp(math.log(1.0) - 2.3025851 * jax.random.uniform(key_of[4], (REPLICAS, LAYERS, ROWS, D), jnp.float32) ** steps_of(key_of[4], (REPLICAS, LAYERS, ROWS, D), ((0, 16), (3, 2)), -0.2, 0.2)), 0.1, 1.0),
        "grad_parts": draw_grad_parts(jax.random.fold_in(key_of[6], 71), 0),
    }


beta_one = 0.9
beta_two = 0.95
correct_one = 0.99997343860111
correct_two = 0.994079470779666
adam_eps = 1e-08
inner_rate = 0.1
decay_rate = 0.1
outer_rate = 0.7
outer_mu = 0.9

def inner_update(weights, anchor_now, first_now, second_now, gradient):
    first_new = beta_one * first_now + (1.0 - beta_one) * gradient
    second_new = beta_two * second_now + (1.0 - beta_two) * gradient * gradient
    update = first_new / correct_one / (jnp.sqrt(second_new / correct_two) + adam_eps)
    stepped = weights - inner_rate * (update + decay_rate * weights)
    return (first_new, second_new, anchor_now - stepped)

def outer_update(mean_delta, moment_now, anchor_now):
    moment_new = outer_mu * moment_now + mean_delta
    anchor_new = anchor_now - outer_rate * (mean_delta + outer_mu * moment_new)
    return (moment_new, anchor_new)

def reference(inner_weights, anchor, outer_moment, adam_first, adam_second, grad_parts):
    gradient = lax.optimization_barrier(jnp.sum(grad_parts.astype(jnp.float32), axis=1))
    first_new, second_new, pseudo = inner_update(inner_weights, anchor[None], adam_first, adam_second, gradient)
    summed = lax.optimization_barrier(jnp.sum(pseudo, axis=0))
    moment_new, anchor_new = outer_update(summed / REPLICAS, outer_moment, anchor)
    return (anchor_new.astype(jnp.bfloat16), anchor_new, moment_new, first_new, second_new)
```

```python
import functools

import jax
import jax.numpy as jnp
from jax import lax
from jax.experimental import pallas as pl
from jax.experimental.pallas import tpu as pltpu
from jax.sharding import PartitionSpec as P

MESH = pl.DeviceIdType.MESH
LANE = 128
SKEW = 2

beta_one = 0.9
beta_two = 0.95
correct_one = 0.99997343860111
correct_two = 0.994079470779666
adam_eps = 1e-08
inner_rate = 0.1
decay_rate = 0.1
outer_rate = 0.7
outer_mu = 0.9


def inner_update(weights, anchor_now, first_now, second_now, gradient):
    first_new = beta_one * first_now + (1.0 - beta_one) * gradient
    second_new = beta_two * second_now + (1.0 - beta_two) * gradient * gradient
    update = first_new / correct_one / (jnp.sqrt(second_new / correct_two) + adam_eps)
    stepped = weights - inner_rate * (update + decay_rate * weights)
    return (first_new, second_new, anchor_now - stepped)


def outer_update(mean_delta, moment_now, anchor_now):
    moment_new = outer_mu * moment_now + mean_delta
    anchor_new = anchor_now - outer_rate * (mean_delta + outer_mu * moment_new)
    return (moment_new, anchor_new)


def plan(cols, workers):
    tiles = cols // LANE
    pipes = tiles
    while pipes % 2 == 0:
        pipes //= 2
    width = cols // pipes
    steps = workers.bit_length() - 1
    halvings, size = 0, width
    while halvings < steps and size % (2 * LANE) == 0:
        size //= 2
        halvings += 1
    return pipes, width, halvings, steps


def kernel(n, workers, pipes, width, halvings, steps, *refs):
    (w_h, a_h, m_h, f_h, s_h, g_h, fresh_o, anchor_o, moment_o, first_o, second_o) = refs[:11]
    (w_v, a_v, m_v, f_v, s_v, g_v, g_r, first_v, second_v, acc, tot, anew, mnew, fresh) = refs[11:25]
    (in_sem, out_sem, gs, gr, rs, rr, ags, agr, fs, fr, ws, wr) = refs[25:37]
    parts = refs[37:]
    cols = w_v.shape[-1]
    me = lax.axis_index("replica")
    mine = lax.axis_index("fsdp")

    def bit_of(b):
        return (me // 2**b) % 2

    def partner(b):
        return me + 2**b * (1 - 2 * bit_of(b))

    def at(ref, off, size):
        return ref.at[:, :, pl.ds(pl.multiple_of(off, LANE), size)]

    loads, grads = [], []
    for q in range(pipes):
        row = []
        for i, (src, dst) in enumerate(
            ((f_h, f_v), (s_h, s_v), (w_h, w_v), (a_h, a_v), (m_h, m_v))
        ):
            row.append(pltpu.make_async_copy(at(src, q * width, width), at(dst, q * width, width), in_sem.at[q, i]))
        row.append(
            pltpu.make_async_copy(at(g_h, mine * cols + q * width, width), at(g_v, q * width, width), in_sem.at[q, 5])
        )
        loads.append(row)
        row = []
        for s in range(1, n):
            peer = lax.rem(mine + s, n)
            row.append(
                pltpu.make_async_remote_copy(
                    src_ref=at(g_h, peer * cols + q * width, width),
                    dst_ref=at(g_r.at[s - 1], q * width, width),
                    send_sem=gs.at[q, s - 1],
                    recv_sem=gr.at[q, s - 1],
                    device_id={"fsdp": peer},
                    device_id_type=MESH,
                )
            )
        grads.append(row)

    barrier = pltpu.get_barrier_semaphore()
    for s in range(1, n):
        pl.semaphore_signal(barrier, inc=1, device_id={"fsdp": lax.rem(mine + s, n)}, device_id_type=MESH)
    for b in range(steps):
        pl.semaphore_signal(barrier, inc=1, device_id={"replica": partner(b)}, device_id_type=MESH)
    for row in loads:
        for copy in row:
            copy.start()
    pl.semaphore_wait(barrier, n - 1 + steps)
    for row in grads:
        for copy in row:
            copy.start()

    sent, stores = [], []

    def store(src, dst, q, i):
        copy = pltpu.make_async_copy(src, dst, out_sem.at[q, i])
        copy.start()
        stores.append(copy)

    def outer(off, size):
        @pl.loop(0, size // LANE)
        def _(j):
            c = pl.ds(pl.multiple_of(off + j * LANE, LANE), LANE)
            moment_new, anchor_new = outer_update(tot[:, :, c] / workers, m_v[:, :, c], a_v[:, :, c])
            mnew[:, :, c] = moment_new
            anew[:, :, c] = anchor_new
            d = pl.ds(pl.multiple_of(mine * cols + off + j * LANE, LANE), LANE)
            fresh[:, :, d] = anchor_new.astype(fresh.dtype)

    def pipe(q):
        base = q * width
        for copy in loads[q]:
            copy.wait()
        for copy in grads[q]:
            copy.wait_recv()
            sent.append(copy)

        @pl.loop(0, width // LANE)
        def _(j):
            c = pl.ds(pl.multiple_of(base + j * LANE, LANE), LANE)
            gradient = g_v[:, :, c].astype(jnp.float32)
            for s in range(n - 1):
                gradient = gradient + g_r[s, :, :, c].astype(jnp.float32)
            first_new, second_new, pseudo = inner_update(
                w_v[:, :, c], a_v[:, :, c], f_v[:, :, c], s_v[:, :, c], gradient
            )
            first_v[:, :, c] = first_new
            second_v[:, :, c] = second_new
            acc[:, :, c] = pseudo

        store(at(first_v, base, width), at(first_o, base, width), q, 0)
        store(at(second_v, base, width), at(second_o, base, width), q, 1)

        off, size = base, width
        offs = [off]
        for b in range(steps):
            if b < halvings:
                size //= 2
                give = off + (1 - bit_of(b)) * size
                off = off + bit_of(b) * size
                offs.append(off)
            else:
                give = off
            copy = pltpu.make_async_remote_copy(
                src_ref=at(acc, give, size),
                dst_ref=at(parts[b], q * size, size),
                send_sem=rs.at[q, b],
                recv_sem=rr.at[q, b],
                device_id={"replica": partner(b)},
                device_id_type=MESH,
            )
            copy.start()
            yield
            if b < halvings:
                copy.wait_recv()
                sent.append(copy)
            else:
                copy.wait()
            into = tot if b == steps - 1 else acc

            @pl.loop(0, size // LANE)
            def _(j, b=b, off=off, size=size, into=into):
                c = pl.ds(pl.multiple_of(off + j * LANE, LANE), LANE)
                d = pl.ds(pl.multiple_of(q * size + j * LANE, LANE), LANE)
                into[:, :, c] = acc[:, :, c] + parts[b][:, :, d]

        for b in reversed(range(halvings)):
            copy = pltpu.make_async_remote_copy(
                src_ref=at(tot, off, size),
                dst_ref=at(tot, off, size),
                send_sem=ags.at[q, b],
                recv_sem=agr.at[q, b],
                device_id={"replica": partner(b)},
                device_id_type=MESH,
            )
            copy.start()
            sent.append(copy)
            if b == 0:
                outer(off, size)
                fresh_out = []
                for s in range(1, n):
                    out = pltpu.make_async_remote_copy(
                        src_ref=at(fresh, mine * cols + off, size),
                        dst_ref=at(fresh, mine * cols + off, size),
                        send_sem=fs.at[q, s - 1],
                        recv_sem=fr.at[q, s - 1],
                        device_id={"fsdp": lax.rem(mine + s, n)},
                        device_id_type=MESH,
                    )
                    out.start()
                    sent.append(out)
                    fresh_out.append(out)
                half_off, half = off, size
            yield
            copy.wait_recv()
            off = offs[b]
            size *= 2
        outer(base + (1 - bit_of(0)) * half, half)
        store(at(mnew, base, width), at(moment_o, base, width), q, 2)
        store(at(anew, base, width), at(anchor_o, base, width), q, 3)
        store(at(fresh, mine * cols + base, width), at(fresh_o, mine * cols + base, width), q, 4)
        yield
        passed = []
        for s in range(1, n):
            fresh_out[s - 1].wait_recv()
            place = lax.rem(mine + n - s, n) * cols + half_off
            copy = pltpu.make_async_remote_copy(
                src_ref=at(fresh, place, half),
                dst_ref=at(fresh, place, half),
                send_sem=ws.at[q, s - 1],
                recv_sem=wr.at[q, s - 1],
                device_id={"replica": partner(0)},
                device_id_type=MESH,
            )
            copy.start()
            sent.append(copy)
            passed.append(copy)
        yield
        for s in range(1, n):
            passed[s - 1].wait_recv()
            place = lax.rem(mine + n - s, n) * cols + base
            store(at(fresh, place, width), at(fresh_o, place, width), q, 4 + s)

    live = [pipe(q) for q in range(pipes)]
    turn = 0
    while any(p is not None for p in live):
        for q in range(pipes):
            if live[q] is not None and turn >= q * SKEW:
                try:
                    next(live[q])
                except StopIteration:
                    live[q] = None
        turn += 1
    for copy in sent:
        copy.wait_send()
    for copy in stores:
        copy.wait()


def solution(mesh):
    n, workers = mesh.shape["fsdp"], mesh.shape["replica"]

    def per_device(inner_weights, anchor, outer_moment, adam_first, adam_second, grad_parts):
        layers, rows, cols = anchor.shape
        pipes, width, halvings, steps = plan(cols, workers)
        shard, whole = (layers, rows, cols), (layers, rows, n * cols)
        f32, bf16 = jnp.float32, jnp.bfloat16
        parts = [
            pltpu.VMEM((layers, rows, pipes * (width >> min(b + 1, halvings))), f32) for b in range(steps)
        ]
        dma = pltpu.SemaphoreType.DMA
        fresh_weights, anchor_new, moment_new, first_new, second_new = pl.pallas_call(
            functools.partial(kernel, n, workers, pipes, width, halvings, steps),
            out_shape=(
                jax.ShapeDtypeStruct(whole, bf16),
                jax.ShapeDtypeStruct(shard, f32),
                jax.ShapeDtypeStruct(shard, f32),
                jax.ShapeDtypeStruct(shard, f32),
                jax.ShapeDtypeStruct(shard, f32),
            ),
            in_specs=[pl.BlockSpec(memory_space=pl.ANY)] * 6,
            out_specs=[pl.BlockSpec(memory_space=pl.ANY)] * 5,
            scratch_shapes=[pltpu.VMEM(shard, f32)] * 5
            + [pltpu.VMEM(shard, bf16), pltpu.VMEM((n - 1,) + shard, bf16)]
            + [pltpu.VMEM(shard, f32)] * 6
            + [pltpu.VMEM(whole, bf16)]
            + [
                dma((pipes, 6)),
                dma((pipes, 4 + n)),
                dma((pipes, n - 1)),
                dma((pipes, n - 1)),
                dma((pipes, steps)),
                dma((pipes, steps)),
                dma((pipes, halvings)),
                dma((pipes, halvings)),
                dma((pipes, n - 1)),
                dma((pipes, n - 1)),
                dma((pipes, n - 1)),
                dma((pipes, n - 1)),
            ]
            + parts,
            compiler_params=pltpu.CompilerParams(collective_id=0, has_side_effects=True),
        )(inner_weights[0], anchor, outer_moment, adam_first[0], adam_second[0], grad_parts[0, 0])
        return (fresh_weights, anchor_new, moment_new, first_new[None], second_new[None])

    in_specs = (
        P("replica", None, None, "fsdp"),
        P(None, None, "fsdp"),
        P(None, None, "fsdp"),
        P("replica", None, None, "fsdp"),
        P("replica", None, None, "fsdp"),
        P("replica", "fsdp", None, None, None),
    )
    out_specs = (
        P(),
        P(None, None, "fsdp"),
        P(None, None, "fsdp"),
        P("replica", None, None, "fsdp"),
        P("replica", None, None, "fsdp"),
    )
    return jax.shard_map(
        per_device, mesh=mesh, in_specs=in_specs, out_specs=out_specs, check_vma=False
    )
```

```python
import functools

import jax
import jax.numpy as jnp
from jax import lax
from jax.experimental import pallas as pl
from jax.experimental.pallas import tpu as pltpu
from jax.sharding import PartitionSpec as P

MESH = pl.DeviceIdType.MESH
LANE = 128
CHUNK = 512
SKEW = 0

beta_one = 0.9
beta_two = 0.95
correct_one = 0.99997343860111
correct_two = 0.994079470779666
adam_eps = 1e-08
inner_rate = 0.1
decay_rate = 0.1
outer_rate = 0.7
outer_mu = 0.9


def inner_update(weights, anchor_now, first_now, second_now, gradient):
    first_new = beta_one * first_now + (1.0 - beta_one) * gradient
    second_new = beta_two * second_now + (1.0 - beta_two) * gradient * gradient
    update = first_new / (jnp.sqrt(second_new) * (correct_one / correct_two**0.5) + correct_one * adam_eps)
    stepped = weights - inner_rate * (update + decay_rate * weights)
    return (first_new, second_new, anchor_now - stepped)


def outer_update(mean_delta, moment_now, anchor_now):
    moment_new = outer_mu * moment_now + mean_delta
    anchor_new = anchor_now - outer_rate * (mean_delta + outer_mu * moment_new)
    return (moment_new, anchor_new)


def plan(cols, workers):
    tiles = cols // LANE
    pipes = tiles
    while pipes % 2 == 0:
        pipes //= 2
    width = cols // pipes
    steps = workers.bit_length() - 1
    halvings, size = 0, width
    while halvings < steps and size % (2 * LANE) == 0:
        size //= 2
        halvings += 1
    return pipes, width, halvings, steps


def sweep(size, body):
    step = size
    while step > CHUNK:
        step //= 2
    if step == size:
        body(0, size)
    else:

        @pl.loop(0, size // step)
        def _(j):
            body(j * step, step)


def kernel(n, workers, pipes, width, halvings, steps, *refs):
    (w_h, a_h, m_h, f_h, s_h, g_h, fresh_o, anchor_o, moment_o, first_o, second_o) = refs[:11]
    (w_v, a_v, m_v, f_v, s_v, g_v, g_r, acc, tot, fresh) = refs[11:21]
    (in_sem, out_sem, gs, gr, rs, rr, ags, agr, fs, fr, ws, wr) = refs[21:33]
    parts = refs[33:]
    layers, _, cols = w_v.shape
    groups, pipes = pipes, layers * pipes
    me = lax.axis_index("replica")
    mine = lax.axis_index("fsdp")

    def bit_of(b):
        return (me // 2**b) % 2

    def partner(b):
        return me + 2**b * (1 - 2 * bit_of(b))

    def at(ref, layer, off, size):
        return ref.at[layer, :, pl.ds(pl.multiple_of(off, LANE), size)]

    loads, grads = [], []
    for q in range(pipes):
        layer, base = q // groups, q % groups * width
        row = []
        for i, (src, dst) in enumerate(
            ((f_h, f_v), (s_h, s_v), (w_h, w_v), (a_h, a_v), (m_h, m_v))
        ):
            row.append(pltpu.make_async_copy(at(src, layer, base, width), at(dst, layer, base, width), in_sem.at[q, i]))
        row.append(
            pltpu.make_async_copy(at(g_h, layer, mine * cols + base, width), at(g_v, layer, base, width), in_sem.at[q, 5])
        )
        loads.append(row)
        row = []
        for s in range(1, n):
            peer = lax.rem(mine + s, n)
            row.append(
                pltpu.make_async_remote_copy(
                    src_ref=at(g_h, layer, peer * cols + base, width),
                    dst_ref=at(g_r.at[s - 1], layer, base, width),
                    send_sem=gs.at[q, s - 1],
                    recv_sem=gr.at[q, s - 1],
                    device_id={"fsdp": peer},
                    device_id_type=MESH,
                )
            )
        grads.append(row)

    barrier = pltpu.get_barrier_semaphore()
    for s in range(1, n):
        pl.semaphore_signal(barrier, inc=1, device_id={"fsdp": lax.rem(mine + s, n)}, device_id_type=MESH)
    for b in range(steps):
        pl.semaphore_signal(barrier, inc=1, device_id={"replica": partner(b)}, device_id_type=MESH)
    for row in loads:
        for copy in row:
            copy.start()
    pl.semaphore_wait(barrier, n - 1 + steps)
    for row in grads:
        for copy in row:
            copy.start()

    sent = []

    def outer(layer, off, size):
        def block(j, wide):
            c = pl.ds(pl.multiple_of(off + j, LANE), wide)
            moment_new, anchor_new = outer_update(tot[layer, :, c] * (1.0 / workers), m_v[layer, :, c], a_v[layer, :, c])
            moment_o[layer, :, c] = moment_new
            anchor_o[layer, :, c] = anchor_new
            d = pl.ds(pl.multiple_of(mine * cols + off + j, LANE), wide)
            fresh[layer, :, d] = anchor_new.astype(fresh.dtype)

        sweep(size, block)

    def pipe(q):
        layer, base = q // groups, q % groups * width
        slot = q % groups
        for copy in loads[q]:
            copy.wait()
        for copy in grads[q]:
            copy.wait_recv()
            sent.append(copy)

        def block(j, wide):
            c = pl.ds(pl.multiple_of(base + j, LANE), wide)
            gradient = g_v[layer, :, c].astype(jnp.float32)
            for s in range(n - 1):
                gradient = gradient + g_r[s, layer, :, c].astype(jnp.float32)
            first_new, second_new, pseudo = inner_update(
                w_v[layer, :, c], a_v[layer, :, c], f_v[layer, :, c], s_v[layer, :, c], gradient
            )
            first_o[layer, :, c] = first_new
            second_o[layer, :, c] = second_new
            acc[layer, :, c] = pseudo

        sweep(width, block)

        off, size = base, width
        offs = [off]
        for b in range(steps):
            if b < halvings:
                size //= 2
                give = off + (1 - bit_of(b)) * size
                off = off + bit_of(b) * size
                offs.append(off)
            else:
                give = off
            copy = pltpu.make_async_remote_copy(
                src_ref=at(acc, layer, give, size),
                dst_ref=at(parts[b], layer, slot * size, size),
                send_sem=rs.at[q, b],
                recv_sem=rr.at[q, b],
                device_id={"replica": partner(b)},
                device_id_type=MESH,
            )
            copy.start()
            yield
            if b < halvings:
                copy.wait_recv()
                sent.append(copy)
            else:
                copy.wait()
            into = tot if b == steps - 1 else acc

            def add(j, wide, b=b, off=off, size=size, into=into):
                c = pl.ds(pl.multiple_of(off + j, LANE), wide)
                d = pl.ds(pl.multiple_of(slot * size + j, LANE), wide)
                into[layer, :, c] = acc[layer, :, c] + parts[b][layer, :, d]

            sweep(size, add)

        for b in reversed(range(halvings)):
            copy = pltpu.make_async_remote_copy(
                src_ref=at(tot, layer, off, size),
                dst_ref=at(tot, layer, off, size),
                send_sem=ags.at[q, b],
                recv_sem=agr.at[q, b],
                device_id={"replica": partner(b)},
                device_id_type=MESH,
            )
            copy.start()
            sent.append(copy)
            if b == 0:
                outer(layer, off, size)
                fresh_out = []
                for s in range(1, n):
                    out = pltpu.make_async_remote_copy(
                        src_ref=at(fresh, layer, mine * cols + off, size),
                        dst_ref=at(fresh, layer, mine * cols + off, size),
                        send_sem=fs.at[q, s - 1],
                        recv_sem=fr.at[q, s - 1],
                        device_id={"fsdp": lax.rem(mine + s, n)},
                        device_id_type=MESH,
                    )
                    out.start()
                    sent.append(out)
                    fresh_out.append(out)
                half_off, half = off, size
            yield
            copy.wait_recv()
            off = offs[b]
            size *= 2
        outer(layer, base + (1 - bit_of(0)) * half, half)
        yield
        passed = []
        for s in range(1, n):
            fresh_out[s - 1].wait_recv()
            place = lax.rem(mine + n - s, n) * cols + half_off
            copy = pltpu.make_async_remote_copy(
                src_ref=at(fresh, layer, place, half),
                dst_ref=at(fresh, layer, place, half),
                send_sem=ws.at[q, s - 1],
                recv_sem=wr.at[q, s - 1],
                device_id={"replica": partner(0)},
                device_id_type=MESH,
            )
            copy.start()
            sent.append(copy)
            passed.append(copy)
        yield
        for copy in passed:
            copy.wait_recv()

    live = [pipe(q) for q in range(pipes)]
    turn = 0
    while any(p is not None for p in live):
        for q in range(pipes):
            if live[q] is not None and turn >= q * SKEW:
                try:
                    next(live[q])
                except StopIteration:
                    live[q] = None
        turn += 1
    for copy in sent:
        copy.wait_send()
    copy = pltpu.make_async_copy(fresh, fresh_o, out_sem)
    copy.start()
    copy.wait()


def put_out(*refs):
    count = len(refs) // 2
    sem = refs[-1]
    copies = [pltpu.make_async_copy(refs[i], refs[count + i], sem.at[i]) for i in range(count)]
    for copy in copies:
        copy.start()
    for copy in copies:
        copy.wait()


def solution(mesh):
    n, workers = mesh.shape["fsdp"], mesh.shape["replica"]

    def per_device(inner_weights, anchor, outer_moment, adam_first, adam_second, grad_parts):
        layers, rows, cols = anchor.shape
        pipes, width, halvings, steps = plan(cols, workers)
        shard, whole = (layers, rows, cols), (layers, rows, n * cols)
        f32, bf16 = jnp.float32, jnp.bfloat16
        parts = [
            pltpu.VMEM((layers, rows, pipes * (width >> min(b + 1, halvings))), f32) for b in range(steps)
        ]
        dma = pltpu.SemaphoreType.DMA
        total = layers * pipes
        outs = [jax.ShapeDtypeStruct(whole, bf16)] + [jax.ShapeDtypeStruct(shard, f32)] * 4
        limit = 67043328 - 2**18 - sum(o.size * o.dtype.itemsize for o in outs)
        results = pl.pallas_call(
            functools.partial(kernel, n, workers, pipes, width, halvings, steps),
            out_shape=[pltpu.VMEM(o.shape, o.dtype) for o in outs],
            in_specs=[pl.BlockSpec(memory_space=pltpu.HBM)] * 6,
            out_specs=[pl.BlockSpec(memory_space=pltpu.VMEM)] * 5,
            scratch_shapes=[pltpu.VMEM(shard, f32)] * 5
            + [pltpu.VMEM(shard, bf16), pltpu.VMEM((n - 1,) + shard, bf16)]
            + [pltpu.VMEM(shard, f32)] * 2
            + [pltpu.VMEM(whole, bf16)]
            + [dma((total, 6)), dma(())]
            + [dma((total, n - 1))] * 2
            + [dma((total, steps))] * 2
            + [dma((total, halvings))] * 2
            + [dma((total, n - 1))] * 4
            + parts,
            compiler_params=pltpu.CompilerParams(collective_id=0, has_side_effects=True, vmem_limit_bytes=limit),
        )(inner_weights[0], anchor, outer_moment, adam_first[0], adam_second[0], grad_parts[0, 0])
        fresh_weights, anchor_new, moment_new, first_new, second_new = pl.pallas_call(
            put_out,
            out_shape=outs,
            in_specs=[pl.BlockSpec(memory_space=pltpu.VMEM)] * 5,
            out_specs=[pl.BlockSpec(memory_space=pl.ANY)] * 5,
            scratch_shapes=[dma((5,))],
            compiler_params=pltpu.CompilerParams(vmem_limit_bytes=2**24),
        )(*results)
        return (fresh_weights, anchor_new, moment_new, first_new[None], second_new[None])

    in_specs = (
        P("replica", None, None, "fsdp"),
        P(None, None, "fsdp"),
        P(None, None, "fsdp"),
        P("replica", None, None, "fsdp"),
        P("replica", None, None, "fsdp"),
        P("replica", "fsdp", None, None, None),
    )
    out_specs = (
        P(),
        P(None, None, "fsdp"),
        P(None, None, "fsdp"),
        P("replica", None, None, "fsdp"),
        P("replica", None, None, "fsdp"),
    )
    return jax.shard_map(
        per_device, mesh=mesh, in_specs=in_specs, out_specs=out_specs, check_vma=False
    )
```

```python
import functools

import jax
import jax.numpy as jnp
from jax import lax
from jax.experimental import pallas as pl
from jax.experimental.pallas import tpu as pltpu
from jax.sharding import PartitionSpec as P

MESH = pl.DeviceIdType.MESH
LANE = 128
CHUNK = 512
SKEW = 0

beta_one = 0.9
beta_two = 0.95
correct_one = 0.99997343860111
correct_two = 0.994079470779666
adam_eps = 1e-08
inner_rate = 0.1
decay_rate = 0.1
outer_rate = 0.7
outer_mu = 0.9


def inner_update(weights, anchor_now, first_now, second_now, gradient):
    first_new = beta_one * first_now + (1.0 - beta_one) * gradient
    second_new = beta_two * second_now + (1.0 - beta_two) * gradient * gradient
    update = first_new / (jnp.sqrt(second_new) * (correct_one / correct_two**0.5) + correct_one * adam_eps)
    stepped = weights - inner_rate * (update + decay_rate * weights)
    return (first_new, second_new, anchor_now - stepped)


def outer_update(mean_delta, moment_now, anchor_now):
    moment_new = outer_mu * moment_now + mean_delta
    anchor_new = anchor_now - outer_rate * (mean_delta + outer_mu * moment_new)
    return (moment_new, anchor_new)


def plan(cols, workers):
    tiles = cols // LANE
    pipes = tiles
    while pipes % 2 == 0:
        pipes //= 2
    width = cols // pipes
    steps = workers.bit_length() - 1
    halvings, size = 0, width
    while halvings < steps and size % (2 * LANE) == 0:
        size //= 2
        halvings += 1
    return pipes, width, halvings, steps


def sweep(size, body):
    step = size
    while step > CHUNK:
        step //= 2
    if step == size:
        body(0, size)
    else:

        @pl.loop(0, size // step)
        def _(j):
            body(j * step, step)


def kernel(n, workers, pipes, width, halvings, steps, *refs):
    (w_h, a_h, m_h, f_h, s_h, g_h, fresh_o, anchor_o, moment_o, first_o, second_o) = refs[:11]
    (w_v, a_v, m_v, f_v, s_v, g_v, g_r, acc, tot, fresh) = refs[11:21]
    (in_sem, out_sem, gs, gr, rs, rr, ags, agr, fs, fr, ws, wr) = refs[21:33]
    parts = refs[33:]
    layers, _, cols = w_v.shape
    groups, pipes = pipes, layers * pipes
    me = lax.axis_index("replica")
    mine = lax.axis_index("fsdp")

    def bit_of(b):
        return (me // 2**b) % 2

    def partner(b):
        return me + 2**b * (1 - 2 * bit_of(b))

    def at(ref, layer, off, size):
        return ref.at[layer, :, pl.ds(pl.multiple_of(off, LANE), size)]

    loads, grads = [], []
    for q in range(pipes):
        layer, base = q // groups, q % groups * width
        row = []
        for i, (src, dst) in enumerate(
            ((f_h, f_v), (s_h, s_v), (w_h, w_v), (a_h, a_v), (m_h, m_v))
        ):
            row.append(pltpu.make_async_copy(at(src, layer, base, width), at(dst, layer, base, width), in_sem.at[q, i]))
        row.append(
            pltpu.make_async_copy(at(g_h, layer, mine * cols + base, width), at(g_v, layer, base, width), in_sem.at[q, 5])
        )
        loads.append(row)
        row = []
        for s in range(1, n):
            peer = lax.rem(mine + s, n)
            row.append(
                pltpu.make_async_remote_copy(
                    src_ref=at(g_h, layer, peer * cols + base, width),
                    dst_ref=at(g_r.at[s - 1], layer, base, width),
                    send_sem=gs.at[q, s - 1],
                    recv_sem=gr.at[q, s - 1],
                    device_id={"fsdp": peer},
                    device_id_type=MESH,
                )
            )
        grads.append(row)

    barrier = pltpu.get_barrier_semaphore()
    for s in range(1, n):
        pl.semaphore_signal(barrier, inc=1, device_id={"fsdp": lax.rem(mine + s, n)}, device_id_type=MESH)
    for b in range(steps):
        pl.semaphore_signal(barrier, inc=1, device_id={"replica": partner(b)}, device_id_type=MESH)
    quad = halvings >= 3
    place4 = (me // 2) % 4
    if quad:
        far = partner(1) + partner(2) - me
        pl.semaphore_signal(barrier, inc=1, device_id={"replica": far}, device_id_type=MESH)
    for row in loads:
        for copy in row:
            copy.start()
    pl.semaphore_wait(barrier, n - 1 + steps + (1 if quad else 0))
    for row in grads:
        for copy in row:
            copy.start()

    sent = []

    def outer(layer, off, size):
        def block(j, wide):
            c = pl.ds(pl.multiple_of(off + j, LANE), wide)
            moment_new, anchor_new = outer_update(tot[layer, :, c] * (1.0 / workers), m_v[layer, :, c], a_v[layer, :, c])
            moment_o[layer, :, c] = moment_new
            anchor_o[layer, :, c] = anchor_new
            d = pl.ds(pl.multiple_of(mine * cols + off + j, LANE), wide)
            fresh[layer, :, d] = anchor_new.astype(fresh.dtype)

        sweep(size, block)

    def pipe(q):
        layer, base = q // groups, q % groups * width
        slot = q % groups
        for copy in loads[q]:
            copy.wait()
        for copy in grads[q]:
            copy.wait_recv()
            sent.append(copy)

        def block(j, wide):
            c = pl.ds(pl.multiple_of(base + j, LANE), wide)
            gradient = g_v[layer, :, c].astype(jnp.float32)
            for s in range(n - 1):
                gradient = gradient + g_r[s, layer, :, c].astype(jnp.float32)
            first_new, second_new, pseudo = inner_update(
                w_v[layer, :, c], a_v[layer, :, c], f_v[layer, :, c], s_v[layer, :, c], gradient
            )
            first_o[layer, :, c] = first_new
            second_o[layer, :, c] = second_new
            acc[layer, :, c] = pseudo

        sweep(width, block)

        off, size = base, width
        offs = [off]
        for b in range(steps):
            if quad and b == 1:
                size //= 4
                trio = []
                for k in range(1, 4):
                    other = (place4 + k) % 4
                    copy = pltpu.make_async_remote_copy(
                        src_ref=at(acc, layer, off + other * size, size),
                        dst_ref=at(parts[1], layer, (slot * 3 + k - 1) * size, size),
                        send_sem=rs.at[q, steps + k - 1],
                        recv_sem=rr.at[q, steps + k - 1],
                        device_id={"replica": me + 2 * (other - place4)},
                        device_id_type=MESH,
                    )
                    copy.start()
                    trio.append(copy)
                offs.append(off)
                off = off + place4 * size
                offs.append(off)
                yield
                for copy in trio:
                    copy.wait_recv()
                    sent.append(copy)

                def add4(j, wide, off=off, size=size):
                    c = pl.ds(pl.multiple_of(off + j, LANE), wide)
                    total = acc[layer, :, c]
                    for k in range(3):
                        d = pl.ds(pl.multiple_of((slot * 3 + k) * size + j, LANE), wide)
                        total = total + parts[1][layer, :, d]
                    (tot if steps == 3 else acc)[layer, :, c] = total

                sweep(size, add4)
                continue
            if quad and b == 2:
                continue
            if b < halvings:
                size //= 2
                give = off + (1 - bit_of(b)) * size
                off = off + bit_of(b) * size
                offs.append(off)
            else:
                give = off
            copy = pltpu.make_async_remote_copy(
                src_ref=at(acc, layer, give, size),
                dst_ref=at(parts[b], layer, slot * size, size),
                send_sem=rs.at[q, b],
                recv_sem=rr.at[q, b],
                device_id={"replica": partner(b)},
                device_id_type=MESH,
            )
            copy.start()
            yield
            if b < halvings:
                copy.wait_recv()
                sent.append(copy)
            else:
                copy.wait()
            into = tot if b == steps - 1 else acc

            def add(j, wide, b=b, off=off, size=size, into=into):
                c = pl.ds(pl.multiple_of(off + j, LANE), wide)
                d = pl.ds(pl.multiple_of(slot * size + j, LANE), wide)
                into[layer, :, c] = acc[layer, :, c] + parts[b][layer, :, d]

            sweep(size, add)

        for b in reversed(range(halvings)):
            if quad and b == 2:
                trio = []
                for k in range(1, 4):
                    other = (place4 + k) % 4
                    copy = pltpu.make_async_remote_copy(
                        src_ref=at(tot, layer, off, size),
                        dst_ref=at(tot, layer, off, size),
                        send_sem=ags.at[q, halvings + k - 1],
                        recv_sem=agr.at[q, halvings + k - 1],
                        device_id={"replica": me + 2 * (other - place4)},
                        device_id_type=MESH,
                    )
                    copy.start()
                    sent.append(copy)
                    trio.append(copy)
                yield
                for copy in trio:
                    copy.wait_recv()
                off = offs[1]
                size *= 4
                continue
            if quad and b == 1:
                continue
            copy = pltpu.make_async_remote_copy(
                src_ref=at(tot, layer, off, size),
                dst_ref=at(tot, layer, off, size),
                send_sem=ags.at[q, b],
                recv_sem=agr.at[q, b],
                device_id={"replica": partner(b)},
                device_id_type=MESH,
            )
            copy.start()
            sent.append(copy)
            if b == 0:
                outer(layer, off, size)
                fresh_out = []
                for s in range(1, n):
                    out = pltpu.make_async_remote_copy(
                        src_ref=at(fresh, layer, mine * cols + off, size),
                        dst_ref=at(fresh, layer, mine * cols + off, size),
                        send_sem=fs.at[q, s - 1],
                        recv_sem=fr.at[q, s - 1],
                        device_id={"fsdp": lax.rem(mine + s, n)},
                        device_id_type=MESH,
                    )
                    out.start()
                    sent.append(out)
                    fresh_out.append(out)
                half_off, half = off, size
            yield
            copy.wait_recv()
            off = offs[b]
            size *= 2
        outer(layer, base + (1 - bit_of(0)) * half, half)
        yield
        passed = []
        for s in range(1, n):
            fresh_out[s - 1].wait_recv()
            place = lax.rem(mine + n - s, n) * cols + half_off
            copy = pltpu.make_async_remote_copy(
                src_ref=at(fresh, layer, place, half),
                dst_ref=at(fresh, layer, place, half),
                send_sem=ws.at[q, s - 1],
                recv_sem=wr.at[q, s - 1],
                device_id={"replica": partner(0)},
                device_id_type=MESH,
            )
            copy.start()
            sent.append(copy)
            passed.append(copy)
        yield
        for copy in passed:
            copy.wait_recv()

    live = [pipe(q) for q in range(pipes)]
    turn = 0
    while any(p is not None for p in live):
        for q in range(pipes):
            if live[q] is not None and turn >= q * SKEW:
                try:
                    next(live[q])
                except StopIteration:
                    live[q] = None
        turn += 1
    for copy in sent:
        copy.wait_send()
    copy = pltpu.make_async_copy(fresh, fresh_o, out_sem)
    copy.start()
    copy.wait()


def put_out(*refs):
    count = len(refs) // 2
    sem = refs[-1]
    copies = [pltpu.make_async_copy(refs[i], refs[count + i], sem.at[i]) for i in range(count)]
    for copy in copies:
        copy.start()
    for copy in copies:
        copy.wait()


def solution(mesh):
    n, workers = mesh.shape["fsdp"], mesh.shape["replica"]

    def per_device(inner_weights, anchor, outer_moment, adam_first, adam_second, grad_parts):
        layers, rows, cols = anchor.shape
        pipes, width, halvings, steps = plan(cols, workers)
        shard, whole = (layers, rows, cols), (layers, rows, n * cols)
        f32, bf16 = jnp.float32, jnp.bfloat16
        parts = [
            pltpu.VMEM((layers, rows, pipes * (width >> min(b + 1, halvings))), f32) for b in range(steps)
        ]
        if halvings >= 3:
            parts[1] = pltpu.VMEM((layers, rows, pipes * 3 * (width >> 3)), f32)
        dma = pltpu.SemaphoreType.DMA
        total = layers * pipes
        outs = [jax.ShapeDtypeStruct(whole, bf16)] + [jax.ShapeDtypeStruct(shard, f32)] * 4
        limit = 67043328 - 2**18 - sum(o.size * o.dtype.itemsize for o in outs)
        results = pl.pallas_call(
            functools.partial(kernel, n, workers, pipes, width, halvings, steps),
            out_shape=[pltpu.VMEM(o.shape, o.dtype) for o in outs],
            in_specs=[pl.BlockSpec(memory_space=pltpu.HBM)] * 6,
            out_specs=[pl.BlockSpec(memory_space=pltpu.VMEM)] * 5,
            scratch_shapes=[pltpu.VMEM(shard, f32)] * 5
            + [pltpu.VMEM(shard, bf16), pltpu.VMEM((n - 1,) + shard, bf16)]
            + [pltpu.VMEM(shard, f32)] * 2
            + [pltpu.VMEM(whole, bf16)]
            + [dma((total, 6)), dma(())]
            + [dma((total, n - 1))] * 2
            + [dma((total, steps + 3))] * 2
            + [dma((total, halvings + 3))] * 2
            + [dma((total, n - 1))] * 4
            + parts,
            compiler_params=pltpu.CompilerParams(collective_id=0, has_side_effects=True, vmem_limit_bytes=limit),
        )(inner_weights[0], anchor, outer_moment, adam_first[0], adam_second[0], grad_parts[0, 0])
        fresh_weights, anchor_new, moment_new, first_new, second_new = pl.pallas_call(
            put_out,
            out_shape=outs,
            in_specs=[pl.BlockSpec(memory_space=pltpu.VMEM)] * 5,
            out_specs=[pl.BlockSpec(memory_space=pl.ANY)] * 5,
            scratch_shapes=[dma((5,))],
            compiler_params=pltpu.CompilerParams(vmem_limit_bytes=2**24),
        )(*results)
        return (fresh_weights, anchor_new, moment_new, first_new[None], second_new[None])

    in_specs = (
        P("replica", None, None, "fsdp"),
        P(None, None, "fsdp"),
        P(None, None, "fsdp"),
        P("replica", None, None, "fsdp"),
        P("replica", None, None, "fsdp"),
        P("replica", "fsdp", None, None, None),
    )
    out_specs = (
        P(),
        P(None, None, "fsdp"),
        P(None, None, "fsdp"),
        P("replica", None, None, "fsdp"),
        P("replica", None, None, "fsdp"),
    )
    return jax.shard_map(
        per_device, mesh=mesh, in_specs=in_specs, out_specs=out_specs, check_vma=False
    )
```
